512 devices in a mesh: tm: 64 (over z, x, core), band: 8 (over y).
Axes of the slice: x: 4, y: 8, z: 8, core: 2. Of those that a mesh axis runs over, the one named last changes fastest.
Arguments:
- query_input: bfloat16 [64, 40, 26, 1120], P('tm', 'band'), may hold values from -6 to 6
- key_input: bfloat16 [64, 40, 26, 1120], P('tm', 'band'), may hold values from -8 to 8
- value_input: bfloat16 [64, 40, 26, 1120], P('tm', 'band'), may hold values from -12 to 12
- cotangent: bfloat16 [64, 40, 26, 1120], P('tm', 'band'), may hold values from -6 to 6
- local_kernel_weight: float32 [3, 3, 1120], replicated, may hold values from -2 to 2
Outputs:
- mixed_out: bfloat16 [64, 40, 26, 1120], P('tm', 'band')
- query_grad: bfloat16 [64, 40, 26, 1120], P('tm', 'band')
- key_grad: bfloat16 [64, 40, 26, 1120], P('tm', 'band')
- value_grad: bfloat16 [64, 40, 26, 1120], P('tm', 'band')
- kernel_grad: float32 [3, 3, 1120], replicated
The draws below stay inside these ranges and needn't reach their ends.
All inputs are finite; a program needn't handle non-finite values.
Results may differ from the reference program's by a relative error of at most 0.018.
Values may be sent and summed in bfloat16 or wider, within the bound.
No kernel may reach another device: no remote copies, remote signals or barrier semaphores. Data moves between devices by JAX's collectives and lax.ppermute only.
A program may use at most 128 MiB of HBM per device.

```python
import jax
import jax.numpy as jnp
from jax import lax

HEADS = 35
HEAD_DIM = 32
D = 1120
FRAME_COLUMNS = 26
FRAMES = 64
FRAME_ROWS = 40
TOKENS = 66560


def token_shape():
    return (FRAMES, FRAME_ROWS, FRAME_COLUMNS, D)


def noise_field(key, shape):
    return jax.random.normal(key, shape, jnp.float32)


def head_factor(key, salt):
    factor = noise_field(jax.random.fold_in(key, salt), (FRAMES, FRAME_ROWS, FRAME_COLUMNS, HEADS, 1))
    return jnp.broadcast_to(factor, (FRAMES, FRAME_ROWS, FRAME_COLUMNS, HEADS, HEAD_DIM)).reshape(token_shape())


def channel_weight(key, salt, lower, upper):
    magnitude = jax.random.uniform(jax.random.fold_in(key, salt), (D,), jnp.float32, lower, upper)
    flipper = jax.random.uniform(jax.random.fold_in(key, salt + 1), (D,), jnp.float32)
    return jnp.where(flipper < 0.5, -magnitude, magnitude)


def frame_offset(key, salt, normal_scale):
    shape = (FRAMES, 1, 1, D)
    return normal_scale * jax.random.normal(jax.random.fold_in(key, salt), shape, jnp.float32)


def draw_key_input(key, part):
    shared = head_factor(key, 5)
    own_noise = noise_field(jax.random.fold_in(key, 11), token_shape())
    offset = frame_offset(key, 12, 1.2)
    return jnp.clip(0.8 * shared + 0.6 * own_noise + offset, -8.0, 8.0).astype(jnp.bfloat16)


def draw_value_input(key, part):
    shared = head_factor(key, 5)
    key_noise = noise_field(jax.random.fold_in(key, 11), token_shape())
    coupling = channel_weight(key, 31, 1.2, 1.8)
    own_noise = noise_field(jax.random.fold_in(key, 23), token_shape())
    offset = frame_offset(key, 24, 2.5)
    total = coupling * shared + 0.8 * key_noise + 0.6 * own_noise + offset
    return jnp.clip(total, -12.0, 12.0).astype(jnp.bfloat16)


def draw_query_input(key, part):
    shared = head_factor(key, 41)
    own_noise = noise_field(jax.random.fold_in(key, 43), token_shape())
    return jnp.clip(1.5 * (0.6 * shared + 0.8 * own_noise), -6.0, 6.0).astype(jnp.bfloat16)


def draw_cotangent(key, part):
    shared = head_factor(key, 41)
    query_noise = noise_field(jax.random.fold_in(key, 43), token_shape())
    coupling = channel_weight(key, 47, 0.6, 1.0)
    own_noise = noise_field(jax.random.fold_in(key, 53), token_shape())
    total = coupling * shared + 0.5 * query_noise + 0.6 * own_noise
    return jnp.clip(total, -6.0, 6.0).astype(jnp.bfloat16)


def centred(stream_key, extent, deviation, bound, held_as=jnp.bfloat16):
    result = deviation * jax.random.normal(stream_key, extent, jnp.float32)
    return jnp.clip(result, min=-bound, max=bound).astype(held_as)


def setup_inputs(seed: int = 0) -> dict:
    seeds = jax.random.split(jax.random.key(seed), 6)
    query_input = draw_query_input(jax.random.fold_in(seeds[5], 71), 0)
    key_input = draw_key_input(jax.random.fold_in(seeds[5], 71), 0)
    value_input = draw_value_input(jax.random.fold_in(seeds[5], 71), 0)
    cotangent = draw_cotangent(jax.random.fold_in(seeds[5], 71), 0)
    local_kernel_weight = centred(seeds[4], (3, 3, D), 9 ** -0.5, 2.0, jnp.float32)
    return {"query_input": query_input, "key_input": key_input, "value_input": value_input, "cotangent": cotangent, "local_kernel_weight": local_kernel_weight}


def feature(x):
    return jnp.where(x > 0, x + 1.0, jnp.exp(jnp.minimum(x, 0.0)))

def slope(x):
    return jnp.where(x > 0, jnp.ones_like(x), jnp.exp(jnp.minimum(x, 0.0)))

def heads_of(x):
    return x.reshape(FRAME_ROWS * FRAME_COLUMNS, HEADS, HEAD_DIM)

def padded_frame_helper(x):
    return jnp.pad(x, ((1, 1), (1, 1), (0, 0)))

def reference(query_input, key_input, value_input, cotangent, local_kernel_weight):
    high = lax.Precision.HIGHEST

    def frame_terms(items):
        query, keyed, value_tensor = items
        key_feat = feature(heads_of(keyed).astype(jnp.float32)).astype(jnp.bfloat16)
        state = jnp.einsum('thd,the->hde', key_feat.astype(jnp.float32), heads_of(value_tensor).astype(jnp.float32), precision=high)
        norm_vec = lax.optimization_barrier(jnp.sum(key_feat.astype(jnp.float32), axis=0))
        return (state, norm_vec)
    frame_state, frame_norm = lax.map(frame_terms, (query_input, key_input, value_input))
    state_all = jnp.cumsum(frame_state, axis=0)
    norm_all = jnp.cumsum(frame_norm, axis=0)

    def frame_forward(items):
        query, value_tensor, grad, state, norm_vec = items
        q_raw = heads_of(query).astype(jnp.float32)
        q_feat = feature(q_raw).astype(jnp.bfloat16).astype(jnp.float32)
        num = jnp.einsum('thd,hde->the', q_feat, state, precision=high)
        den = jnp.einsum('thd,hd->th', q_feat, norm_vec, precision=high)
        attn = num / den[:, :, None]
        value_padded = padded_frame_helper(value_tensor).astype(jnp.float32)
        gpad = padded_frame_helper(grad).astype(jnp.float32)
        local_output = jnp.zeros((FRAME_ROWS, FRAME_COLUMNS, D), jnp.float32)
        v_local = jnp.zeros((FRAME_ROWS, FRAME_COLUMNS, D), jnp.float32)
        gradient_whole = grad.astype(jnp.float32)
        kernel_row_slice = []
        for row_offset in range(3):
            for column_offset in range(3):
                local_output = local_output + local_kernel_weight[row_offset, column_offset] * value_padded[row_offset:row_offset + FRAME_ROWS, column_offset:column_offset + FRAME_COLUMNS]
                v_local = v_local + local_kernel_weight[row_offset, column_offset] * gpad[2 - row_offset:2 - row_offset + FRAME_ROWS, 2 - column_offset:2 - column_offset + FRAME_COLUMNS]
                kernel_row_slice.append(lax.optimization_barrier(jnp.sum(gradient_whole * value_padded[row_offset:row_offset + FRAME_ROWS, column_offset:column_offset + FRAME_COLUMNS], axis=(0, 1))))
        mixed = (attn.reshape(FRAME_ROWS, FRAME_COLUMNS, D) + local_output).astype(jnp.bfloat16)
        g_heads = heads_of(gradient_whole)
        scaled = g_heads / den[:, :, None]
        den_grad = -lax.optimization_barrier(jnp.sum(g_heads * attn, axis=2)) / den
        back_state = jnp.einsum('thd,the->hde', q_feat, scaled, precision=high)
        back_norm = jnp.einsum('thd,th->hd', q_feat, den_grad, precision=high)
        q_grad = jnp.einsum('the,hde->thd', scaled, state, precision=high) + den_grad[:, :, None] * norm_vec[None]
        q_grad = (q_grad * slope(q_raw)).reshape(FRAME_ROWS, FRAME_COLUMNS, D).astype(jnp.bfloat16)
        return (mixed, q_grad, back_state, back_norm, v_local, jnp.stack(kernel_row_slice).reshape(3, 3, D))
    mixed_out, query_grad, back_state, back_norm, v_local, kernel_terms = lax.map(frame_forward, (query_input, value_input, cotangent, state_all, norm_all))
    later_state = jnp.flip(jnp.cumsum(jnp.flip(back_state, 0), axis=0), 0)
    later_norm = jnp.flip(jnp.cumsum(jnp.flip(back_norm, 0), axis=0), 0)

    def frame_backward(items):
        keyed, value_tensor, local_part, state, norm_vec = items
        k_raw = heads_of(keyed).astype(jnp.float32)
        key_feat = feature(k_raw).astype(jnp.bfloat16).astype(jnp.float32)
        k_grad = jnp.einsum('the,hde->thd', heads_of(value_tensor).astype(jnp.float32), state, precision=high) + norm_vec[None]
        k_grad = (k_grad * slope(k_raw)).reshape(FRAME_ROWS, FRAME_COLUMNS, D).astype(jnp.bfloat16)
        v_grad = jnp.einsum('thd,hde->the', key_feat, state, precision=high).reshape(FRAME_ROWS, FRAME_COLUMNS, D) + local_part
        return (k_grad, v_grad.astype(jnp.bfloat16))
    key_grad, value_grad = lax.map(frame_backward, (key_input, value_input, v_local, later_state, later_norm))
    kernel_grad = lax.optimization_barrier(jnp.sum(kernel_terms, axis=0)) / jnp.sqrt(jnp.float32(TOKENS))
    return (mixed_out, query_grad, key_grad, value_grad, kernel_grad)
```

```python
import math

import jax
import jax.numpy as jnp
from jax import lax
from jax.experimental import pallas as pl
from jax.experimental.pallas import tpu as pltpu
from jax.sharding import Mesh
from jax.sharding import PartitionSpec as P

HEADS = 35
HEAD_DIM = 32
LANES = 128
WIDTH = HEADS * HEAD_DIM
GROUPS = -(-WIDTH // LANES)
PAD = 32
CHUNKS = 16
SLOTS = 3
STATE_TILES = 4 * GROUPS
EXTRA = STATE_TILES // SLOTS

f32 = jnp.float32
bf16 = jnp.bfloat16


def span(group):
    start = group * LANES
    return start, min(LANES, WIDTH - start)


def dot(a, b):
    return lax.dot_general(a, b, (((1,), (0,)), ((), ())), preferred_element_type=f32)


def dot_nt(a, b):
    return lax.dot_general(a, b, (((1,), (1,)), ((), ())), preferred_element_type=f32)


def dot_tn(a, b):
    return lax.dot_general(a, b, (((0,), (0,)), ((), ())), preferred_element_type=f32)


def split(x):
    high = x.astype(bf16)
    return high, (x - high.astype(f32)).astype(bf16)


def same_head():
    rows = lax.broadcasted_iota(jnp.int32, (LANES, LANES), 0) // HEAD_DIM
    columns = lax.broadcasted_iota(jnp.int32, (LANES, LANES), 1) // HEAD_DIM
    return rows == columns


def lane_head():
    return lax.broadcasted_iota(jnp.int32, (HEAD_DIM, LANES), 1) // HEAD_DIM


def compact(full, heads):
    out = jnp.zeros((HEAD_DIM, LANES), f32)
    for k in range(LANES // HEAD_DIM):
        out = jnp.where(heads == k, full[k * HEAD_DIM : (k + 1) * HEAD_DIM], out)
    return out


def expand(blocks, same):
    return jnp.where(same, jnp.concatenate([blocks] * (LANES // HEAD_DIM), axis=0), 0.0)


def put_state(send, group, blocks):
    for k in range(4):
        tile = group * 4 + k
        send[tile // SLOTS, pl.ds(8 * (tile % SLOTS), 8), :] = blocks[8 * k : 8 * k + 8]


def get_state(received, group):
    tiles = [group * 4 + k for k in range(4)]
    return jnp.concatenate(
        [received[t // SLOTS, pl.ds(8 * (t % SLOTS), 8), :] for t in tiles], axis=0
    )


def extra_tile(group):
    return EXTRA + group // SLOTS, 8 * (group % SLOTS)


def tail_rows(group):
    return EXTRA + (GROUPS + group // SLOTS) // SLOTS, (
        8 * ((GROUPS + group // SLOTS) % SLOTS) + 2 * (group % SLOTS)
    )


def clear_extra(send):
    for piece in range(EXTRA, CHUNKS):
        send[piece] = jnp.zeros((8 * SLOTS, LANES), f32)


def fill_rows(scratch, ref, rows):
    scratch[...] = jnp.zeros_like(scratch)
    for r in range(rows):
        scratch[r, pl.ds(0, ref.shape[1]), pl.ds(0, WIDTH)] = ref[r]


def state_kernel(k_ref, v_ref, g_ref, send, first, last, k_s, v_s):
    rows, columns = k_ref.shape[0], k_ref.shape[1]
    for n, ref in enumerate((v_ref, g_ref)):
        first[n] = ref[0]
        last[n] = ref[rows - 1]
    fill_rows(k_s, k_ref, rows)
    fill_rows(v_s, v_ref, rows)
    clear_extra(send)
    heads = lane_head()
    token = lax.broadcasted_iota(jnp.int32, (rows, PAD, LANES), 1) < columns
    for group in range(GROUPS):
        lanes = pl.ds(group * LANES, LANES)
        k_raw = k_s[:, :, lanes].astype(f32)
        feat = jnp.where(k_raw > 0, k_raw + 1.0, jnp.exp(jnp.minimum(k_raw, 0.0)))
        feat = jnp.where(token, feat, 0.0).astype(bf16).reshape(rows * PAD, LANES)
        value = v_s[:, :, lanes].reshape(rows * PAD, LANES)
        put_state(send, group, compact(dot_tn(feat, value), heads))
        piece, row = extra_tile(group)
        send[piece, pl.ds(row, 1), :] = jnp.sum(feat.astype(f32), axis=0, keepdims=True)


def totals_kernel(received, pair, send):
    bands = received.shape[0] // 2
    for core in range(2):
        total = received[core * bands]
        for band in range(1, bands):
            total = total + received[core * bands + band]
        pair[core] = total
    whole = pair[0] + pair[1]
    for n in range(send.shape[0]):
        send[n] = whole


def prefix_kernel(place, received, pair, send):
    at = place[0]
    carry = jnp.zeros(pair.shape[1:], f32)
    for n in range(received.shape[0]):
        carry = carry + jnp.where(n < at, received[n], 0.0)
    first = carry + pair[0]
    second = first + pair[1]
    bands = send.shape[0] // 2
    for band in range(bands):
        send[band] = first
        send[bands + band] = second


def suffix_kernel(place, received, pair, send):
    at, piece = place[0], place[1]
    later = jnp.zeros(pair.shape[1:], f32)
    earlier = jnp.zeros(pair.shape[1:], f32)
    for n in range(received.shape[0]):
        later = later + jnp.where(n > at, received[n], 0.0)
        earlier = earlier + jnp.where(n < at, received[n], 0.0)
    row = lax.broadcasted_iota(jnp.int32, pair.shape[1:], 0)
    extra = (piece - EXTRA) * (8 * SLOTS) + row
    norm = jnp.logical_and(extra < 8 * GROUPS, row % 8 == 0)
    summed = jnp.logical_and(piece >= EXTRA, jnp.logical_not(norm))
    second = later + pair[1]
    first = second + pair[0]
    whole = first + earlier
    first = jnp.where(summed, whole, first)
    second = jnp.where(summed, whole, second)
    bands = send.shape[0] // 2
    for band in range(bands):
        send[band] = first
        send[bands + band] = second


def local_kernel(v_ref, g_ref, above, below, w_ref, local, v_local, terms, v_s, g_s):
    rows, columns = v_ref.shape[0], v_ref.shape[1]
    for n, (scratch, ref) in enumerate(((v_s, v_ref), (g_s, g_ref))):
        scratch[...] = jnp.zeros_like(scratch)
        scratch[0, pl.ds(0, columns), pl.ds(0, WIDTH)] = above[n]
        scratch[rows + 1, pl.ds(0, columns), pl.ds(0, WIDTH)] = below[n]
        for r in range(rows):
            scratch[r + 1, pl.ds(0, columns), pl.ds(0, WIDTH)] = ref[r]
    terms[...] = jnp.zeros_like(terms)
    for group in range(GROUPS):
        start, wide = span(group)
        lanes = pl.ds(start, LANES)

        def shifted(scratch):
            out = []
            for r in range(rows + 2):
                here = scratch[r, :, lanes].astype(f32)
                out.append((pltpu.roll(here, 1, 0), here, pltpu.roll(here, PAD - 1, 0)))
            return out

        taps = [
            [jnp.broadcast_to(w_ref[i, pl.ds(j, 1), lanes], (PAD, LANES)) for j in range(3)]
            for i in range(3)
        ]
        value = shifted(v_s)
        for r in range(rows):
            total = jnp.zeros((PAD, LANES), f32)
            for i in range(3):
                for j in range(3):
                    total = total + taps[i][j] * value[r + i][j]
            local[r, :, lanes] = total
        for i in range(3):
            for j in range(3):
                term = jnp.zeros((PAD, LANES), f32)
                for r in range(rows):
                    term = term + g_s[r + 1, :, lanes].astype(f32) * value[r + i][j]
                n = 1 + 3 * i + j
                terms[pl.ds(n, 1), lanes] = jnp.sum(term, axis=0, keepdims=True)
        grad = shifted(g_s)
        for r in range(rows):
            total = jnp.zeros((PAD, LANES), f32)
            for i in range(3):
                for j in range(3):
                    total = total + taps[i][j] * grad[r + 2 - i][2 - j]
            v_local[r, :, lanes] = total


def query_kernel(q_ref, g_ref, received, local, terms, send, mixed, q_grad, q_s, g_s):
    rows, columns = q_ref.shape[0], q_ref.shape[1]
    tokens = rows * PAD
    fill_rows(q_s, q_ref, rows)
    fill_rows(g_s, g_ref, rows)
    clear_extra(send)
    heads, same = lane_head(), same_head()
    ones = same.astype(f32).astype(bf16)
    lane = lax.broadcasted_iota(jnp.int32, (1, LANES), 1)
    for group in range(GROUPS):
        start, wide = span(group)
        lanes = pl.ds(start, LANES)
        q_raw = q_s[:, :, lanes].reshape(tokens, LANES).astype(f32)
        low = jnp.exp(jnp.minimum(q_raw, 0.0))
        feat = jnp.where(q_raw > 0, q_raw + 1.0, low).astype(bf16)
        slope = jnp.where(q_raw > 0, 1.0, low)
        grad = g_s[:, :, lanes].reshape(tokens, LANES)
        high, rest = split(expand(get_state(received, group), same))
        piece, row = extra_tile(group)
        norm = received[piece, pl.ds(row, 1), :]
        norm = jnp.where(lane < wide, norm, 1.0)
        num = dot(feat, high) + dot(feat, rest)
        wide_feat = feat.astype(f32)
        a, b = split(wide_feat * norm)
        inverse = 1.0 / (dot(a, ones) + dot(b, ones))
        attn = num * inverse
        a, b = split(grad.astype(f32) * num)
        along = (dot(a, ones) + dot(b, ones)) * inverse
        back = dot_nt(grad, high) + dot_nt(grad, rest)
        back = (back - along * norm) * inverse * slope
        scaled = wide_feat * inverse
        a, b = split(scaled)
        put_state(send, group, compact(dot_tn(grad, a) + dot_tn(grad, b), heads))
        block = terms[pl.ds(0, 16), lanes]
        back_norm = -jnp.sum(scaled * along, axis=0, keepdims=True)
        send[piece, pl.ds(row, 8), :] = block[0:8]
        send[piece, pl.ds(row, 1), :] = back_norm
        piece, row = tail_rows(group)
        send[piece, pl.ds(row, 2), :] = block[8:10]
        here = attn.reshape(rows, PAD, LANES) + local[:, :, lanes]
        mixed[:, :, pl.ds(start, wide)] = here[:, :columns, :wide].astype(bf16)
        back = back.reshape(rows, PAD, LANES)
        q_grad[:, :, pl.ds(start, wide)] = back[:, :columns, :wide].astype(bf16)


def key_kernel(scale, k_ref, v_ref, received, v_local, k_grad, v_grad, kernel_grad, k_s, v_s):
    rows, columns = k_ref.shape[0], k_ref.shape[1]
    tokens = rows * PAD
    fill_rows(k_s, k_ref, rows)
    fill_rows(v_s, v_ref, rows)
    same = same_head()
    for group in range(GROUPS):
        start, wide = span(group)
        lanes = pl.ds(start, LANES)
        k_raw = k_s[:, :, lanes].reshape(tokens, LANES).astype(f32)
        low = jnp.exp(jnp.minimum(k_raw, 0.0))
        feat = jnp.where(k_raw > 0, k_raw + 1.0, low).astype(bf16)
        slope = jnp.where(k_raw > 0, 1.0, low)
        value = v_s[:, :, lanes].reshape(tokens, LANES)
        high, rest = split(expand(get_state(received, group), same))
        piece, row = extra_tile(group)
        head_rows = received[piece, pl.ds(row, 8), :]
        back = dot(value, high) + dot(value, rest) + head_rows[0:1]
        back = (back * slope).reshape(rows, PAD, LANES)
        k_grad[:, :, pl.ds(start, wide)] = back[:, :columns, :wide].astype(bf16)
        here = (dot_nt(feat, high) + dot_nt(feat, rest)).reshape(rows, PAD, LANES)
        here = here + v_local[:, :, lanes]
        v_grad[:, :, pl.ds(start, wide)] = here[:, :columns, :wide].astype(bf16)
        piece, row = tail_rows(group)
        tail = received[piece, pl.ds(row, 2), :]
        for n in range(9):
            term = head_rows[n + 1 : n + 2] if n < 7 else tail[n - 7 : n - 6]
            kernel_grad[n // 3, pl.ds(n % 3, 1), pl.ds(start, wide)] = (term * scale)[:, :wide]


def call(body, out_shape, name, scratch=(), scalars=0, keep=()):
    def run(*args):
        specs = [
            pl.BlockSpec(memory_space=pltpu.SMEM if n < scalars else pltpu.VMEM)
            for n in range(len(args))
        ]
        args = [
            a if n < scalars else pltpu.with_memory_space_constraint(a, pltpu.VMEM)
            for n, a in enumerate(args)
        ]
        return pl.pallas_call(
            body,
            out_shape=[
                a if n in keep else pltpu.VMEM(a.shape, a.dtype) for n, a in enumerate(out_shape)
            ],
            in_specs=specs,
            out_specs=[pl.BlockSpec(memory_space=pltpu.VMEM)] * len(out_shape),
            scratch_shapes=scratch,
            name=name,
        )(*args)

    return run


def shards(query_input, key_input, value_input, cotangent, local_kernel_weight):
    q, k, v, g = (x[0] for x in (query_input, key_input, value_input, cotangent))
    rows, columns, width = q.shape
    shape = jax.ShapeDtypeStruct
    lanes = GROUPS * LANES
    piece = (8 * SLOTS, LANES)
    planes = lax.axis_size("z") * lax.axis_size("x")
    place = jnp.stack(
        [
            lax.axis_index("z") * lax.axis_size("x") + lax.axis_index("x"),
            lax.axis_index("c") * lax.axis_size("y") + lax.axis_index("y"),
        ]
    ).astype(jnp.int32)
    token_scratch = pltpu.VMEM((rows, PAD, lanes), bf16)
    rim_scratch = pltpu.VMEM((rows + 2, PAD, lanes), bf16)
    tokens = shape(q.shape, bf16)
    padded = shape((rows, PAD, lanes), f32)
    edge = shape((2, columns, width), bf16)
    pieces = shape((CHUNKS, *piece), f32)

    def exchange(x):
        return lax.all_to_all(x, ("c", "y"), 0, 0, tiled=True)

    def across_frames(send, body, name):
        received = exchange(send)
        pair, whole = call(
            totals_kernel, (shape((2, *piece), f32), shape((planes, *piece), f32)), "totals"
        )(received)
        gathered = lax.all_to_all(whole, ("z", "x"), 0, 0, tiled=True)
        (back,) = call(body, (pieces,), name, scalars=1)(place, gathered, pair)
        return exchange(back)

    send, first, last = call(state_kernel, (pieces, edge, edge), "state", [token_scratch] * 2)(
        k, v, g
    )
    ends = lax.axis_size("y") - 1
    above = lax.ppermute(last, "y", [(i, i + 1) for i in range(ends)])
    below = lax.ppermute(first, "y", [(i + 1, i) for i in range(ends)])
    weight = jnp.pad(local_kernel_weight, ((0, 0), (0, 0), (0, lanes - width)))
    state = across_frames(send, prefix_kernel, "prefix")
    local, v_local, terms = call(
        local_kernel, (padded, padded, shape((16, lanes), f32)), "local", [rim_scratch] * 2
    )(v, g, above, below, weight)
    send, mixed, q_grad = call(
        query_kernel, (pieces, tokens, tokens), "query", [token_scratch] * 2, keep=(1, 2)
    )(q, g, state, local, terms)
    later = across_frames(send, suffix_kernel, "suffix")
    count = rows * columns
    for axis in ("z", "x", "c", "y"):
        count = count * lax.axis_size(axis)
    scale = 1.0 / math.sqrt(count)

    def key_body(*refs):
        key_kernel(scale, *refs)

    k_grad, v_grad, kernel_grad = call(
        key_body,
        (tokens, tokens, shape(local_kernel_weight.shape, f32)),
        "key",
        [token_scratch] * 2,
        keep=(0, 1, 2),
    )(k, v, later, v_local)
    return (mixed[None], q_grad[None], k_grad[None], v_grad[None], kernel_grad)


def solution(mesh):
    torus = Mesh(mesh.devices.reshape(8, 4, 2, 8), ("z", "x", "c", "y"))
    tokens = P(("z", "x", "c"), "y", None, None)
    return jax.shard_map(
        shards,
        mesh=torus,
        in_specs=(tokens, tokens, tokens, tokens, P()),
        out_specs=(tokens, tokens, tokens, tokens, P()),
        check_vma=False,
    )
```

```python
import math

import jax
import jax.numpy as jnp
from jax import lax
from jax.experimental import pallas as pl
from jax.experimental.pallas import tpu as pltpu
from jax.sharding import Mesh
from jax.sharding import PartitionSpec as P

HEADS = 35
HEAD_DIM = 32
LANES = 128
WIDTH = HEADS * HEAD_DIM
GROUPS = -(-WIDTH // LANES)
PAD = 32
STATE_ROWS = GROUPS * HEAD_DIM
TAIL_ROW = STATE_ROWS + 8 * GROUPS

f32 = jnp.float32
bf16 = jnp.bfloat16


def span(group):
    start = group * LANES
    return start, min(LANES, WIDTH - start)


def dot(a, b):
    return lax.dot_general(a, b, (((1,), (0,)), ((), ())), preferred_element_type=f32)


def dot_nt(a, b):
    return lax.dot_general(a, b, (((1,), (1,)), ((), ())), preferred_element_type=f32)


def dot_tn(a, b):
    return lax.dot_general(a, b, (((0,), (0,)), ((), ())), preferred_element_type=f32)


def split(x):
    high = x.astype(bf16)
    return high, (x - high.astype(f32)).astype(bf16)


def same_head():
    rows = lax.broadcasted_iota(jnp.int32, (LANES, LANES), 0) // HEAD_DIM
    columns = lax.broadcasted_iota(jnp.int32, (LANES, LANES), 1) // HEAD_DIM
    return rows == columns


def lane_head():
    return lax.broadcasted_iota(jnp.int32, (HEAD_DIM, LANES), 1) // HEAD_DIM


def compact(full, heads):
    out = jnp.zeros((HEAD_DIM, LANES), f32)
    for k in range(LANES // HEAD_DIM):
        out = jnp.where(heads == k, full[k * HEAD_DIM : (k + 1) * HEAD_DIM], out)
    return out


def expand(blocks, same):
    return jnp.where(same, jnp.concatenate([blocks] * (LANES // HEAD_DIM), axis=0), 0.0)


def state_rows(group):
    return pl.ds(group * HEAD_DIM, HEAD_DIM)


def norm_row(group):
    return pl.ds(STATE_ROWS + group, 1)


def head_rows(group, count=8):
    return pl.ds(STATE_ROWS + 8 * group, count)


def tail_rows(group):
    return pl.ds(TAIL_ROW + 2 * group, 2)


def clear_extra(send):
    send[pl.ds(STATE_ROWS, send.shape[0] - STATE_ROWS), :] = jnp.zeros(
        (send.shape[0] - STATE_ROWS, LANES), f32
    )


def fill_rows(scratch, ref, rows):
    scratch[...] = jnp.zeros_like(scratch)
    for r in range(rows):
        scratch[r, pl.ds(0, ref.shape[1]), pl.ds(0, WIDTH)] = ref[r]


def edge_kernel(row, v_ref, g_ref, out):
    for n, ref in enumerate((v_ref, g_ref)):
        out[n] = ref[row]


def state_kernel(k_ref, v_ref, send, k_s, v_s):
    rows, columns = k_ref.shape[0], k_ref.shape[1]
    fill_rows(k_s, k_ref, rows)
    fill_rows(v_s, v_ref, rows)
    clear_extra(send)
    heads = lane_head()
    token = lax.broadcasted_iota(jnp.int32, (rows, PAD, LANES), 1) < columns
    for group in range(GROUPS):
        lanes = pl.ds(group * LANES, LANES)
        k_raw = k_s[:, :, lanes].astype(f32)
        feat = jnp.where(k_raw > 0, k_raw + 1.0, jnp.exp(jnp.minimum(k_raw, 0.0)))
        feat = jnp.where(token, feat, 0.0).astype(bf16).reshape(rows * PAD, LANES)
        value = v_s[:, :, lanes].reshape(rows * PAD, LANES)
        send[state_rows(group), :] = compact(dot_tn(feat, value), heads)
        send[norm_row(group), :] = jnp.sum(feat.astype(f32), axis=0, keepdims=True)


def totals_kernel(received, frames, send):
    count = frames.shape[0]
    bands = received.shape[0] // count
    whole = jnp.zeros(received.shape[1:], f32)
    for frame in range(count):
        total = received[frame * bands]
        for band in range(1, bands):
            total = total + received[frame * bands + band]
        frames[frame] = total
        whole = whole + total
    for n in range(send.shape[0]):
        send[n] = whole


def prefix_kernel(received, frames, send):
    plane = lax.axis_index("z")
    total = jnp.zeros(received.shape[1:], f32)
    for n in range(received.shape[0]):
        total = total + jnp.where(n < plane, received[n], 0.0)
    count = frames.shape[0]
    bands = send.shape[0] // count
    for frame in range(count):
        total = total + frames[frame]
        for band in range(bands):
            send[frame * bands + band] = total


def suffix_kernel(received, frames, send):
    plane = lax.axis_index("z")
    later = jnp.zeros(received.shape[1:], f32)
    whole = jnp.zeros(received.shape[1:], f32)
    for n in range(received.shape[0]):
        later = later + jnp.where(n > plane, received[n], 0.0)
        whole = whole + received[n]
    lane = lax.broadcasted_iota(jnp.int32, received.shape[1:], 1)
    first = lax.axis_index(("x", "c", "y")) * (received.shape[2] // LANES)
    row = first + lane // LANES
    norm = jnp.logical_and(row < TAIL_ROW, (row - STATE_ROWS) % 8 == 0)
    summed = jnp.logical_and(row >= STATE_ROWS, jnp.logical_not(norm))
    count = frames.shape[0]
    bands = send.shape[0] // count
    for frame in reversed(range(count)):
        later = later + frames[frame]
        out = jnp.where(summed, whole, later)
        for band in range(bands):
            send[frame * bands + band] = out


def fill_rim(scratch, ref, above, below=None):
    rows, columns = ref.shape[0], ref.shape[1]
    scratch[...] = jnp.zeros_like(scratch)
    scratch[0, pl.ds(0, columns), pl.ds(0, WIDTH)] = above
    for r in range(rows):
        scratch[r + 1, pl.ds(0, columns), pl.ds(0, WIDTH)] = ref[r]
    if below is not None:
        scratch[rows + 1, pl.ds(0, columns), pl.ds(0, WIDTH)] = below


def shifted(scratch, lanes):
    out = []
    for r in range(scratch.shape[0]):
        here = scratch[r, :, lanes].astype(f32)
        out.append((pltpu.roll(here, 1, 0), here, pltpu.roll(here, PAD - 1, 0)))
    return out


def terms_kernel(v_ref, g_ref, above, terms, v_s, g_s):
    rows = v_ref.shape[0]
    fill_rim(v_s, v_ref, above[0])
    fill_rim(g_s, g_ref, above[1])
    terms[...] = jnp.zeros_like(terms)
    for group in range(GROUPS):
        lanes = pl.ds(group * LANES, LANES)
        value = shifted(v_s, lanes)
        grad = [g_s[r, :, lanes].astype(f32) for r in range(rows + 1)]
        for n in range(9):
            step = n // 3 - 1
            term = jnp.zeros((PAD, LANES), f32)
            for r in range(1 - max(step, 0), rows + 1 - max(step, 0)):
                term = term + grad[r] * value[r + step][n % 3]
            terms[pl.ds(1 + n, 1), lanes] = jnp.sum(term, axis=0, keepdims=True)


def attend(q_s, g_s, received, group, same, ones):
    tokens = q_s.shape[0] * PAD
    wide = span(group)[1]
    lanes = pl.ds(group * LANES, LANES)
    q_raw = q_s[:, :, lanes].reshape(tokens, LANES).astype(f32)
    low = jnp.exp(jnp.minimum(q_raw, 0.0))
    feat = jnp.where(q_raw > 0, q_raw + 1.0, low).astype(bf16)
    slope = jnp.where(q_raw > 0, 1.0, low)
    grad = g_s[:, :, lanes].reshape(tokens, LANES)
    state = split(expand(received[state_rows(group), :], same))
    norm = received[norm_row(group), :]
    norm = jnp.where(lax.broadcasted_iota(jnp.int32, (1, LANES), 1) < wide, norm, 1.0)
    num = dot(feat, state[0]) + dot(feat, state[1])
    a, b = split(feat.astype(f32) * norm)
    inverse = 1.0 / (dot(a, ones) + dot(b, ones))
    a, b = split(grad.astype(f32) * num)
    along = (dot(a, ones) + dot(b, ones)) * inverse
    return feat, slope, grad, state, norm, num, inverse, along


def query_kernel(q_ref, g_ref, received, terms, send, q_s, g_s):
    rows = q_ref.shape[0]
    fill_rows(q_s, q_ref, rows)
    fill_rows(g_s, g_ref, rows)
    clear_extra(send)
    heads, same = lane_head(), same_head()
    ones = same.astype(f32).astype(bf16)
    for group in range(GROUPS):
        feat, _, grad, _, _, _, inverse, along = attend(q_s, g_s, received, group, same, ones)
        scaled = feat.astype(f32) * inverse
        a, b = split(scaled)
        send[state_rows(group), :] = compact(dot_tn(grad, a) + dot_tn(grad, b), heads)
        lanes = pl.ds(group * LANES, LANES)
        send[head_rows(group, 8), :] = terms[pl.ds(0, 8), lanes]
        send[head_rows(group, 1), :] = -jnp.sum(scaled * along, axis=0, keepdims=True)
        send[tail_rows(group), :] = terms[pl.ds(8, 2), lanes]


def grad_kernel(q_ref, g_ref, received, q_grad, attn, q_s, g_s):
    rows, columns = q_ref.shape[0], q_ref.shape[1]
    fill_rows(q_s, q_ref, rows)
    fill_rows(g_s, g_ref, rows)
    same = same_head()
    ones = same.astype(f32).astype(bf16)
    for group in range(GROUPS):
        start, wide = span(group)
        _, slope, grad, state, norm, num, inverse, along = attend(
            q_s, g_s, received, group, same, ones
        )
        back = dot_nt(grad, state[0]) + dot_nt(grad, state[1])
        back = ((back - along * norm) * inverse * slope).reshape(rows, PAD, LANES)
        q_grad[:, :, pl.ds(start, wide)] = back[:, :columns, :wide].astype(bf16)
        attn[:, :, pl.ds(start, LANES)] = (num * inverse).reshape(rows, PAD, LANES)


def mixed_kernel(v_ref, g_ref, above, below, w_ref, attn, mixed, v_local, v_s, g_s):
    rows, columns = v_ref.shape[0], v_ref.shape[1]
    fill_rim(v_s, v_ref, above[0], below[0])
    fill_rim(g_s, g_ref, above[1], below[1])
    for group in range(GROUPS):
        start, wide = span(group)
        lanes = pl.ds(start, LANES)
        taps = [
            jnp.broadcast_to(w_ref[n // 3, pl.ds(n % 3, 1), lanes], (PAD, LANES)) for n in range(9)
        ]
        value, grads = shifted(v_s, lanes), shifted(g_s, lanes)
        for r in range(rows):
            here = jnp.zeros((PAD, LANES), f32)
            there = jnp.zeros((PAD, LANES), f32)
            for n, tap in enumerate(taps):
                here = here + tap * value[r + n // 3][n % 3]
                there = there + tap * grads[r + 2 - n // 3][2 - n % 3]
            v_local[r, :, lanes] = there
            here = attn[r, :, lanes] + here
            mixed[r, :, pl.ds(start, wide)] = here[:columns, :wide].astype(bf16)


def key_kernel(scale, k_ref, v_ref, received, v_local, k_grad, v_grad, kernel_grad, k_s, v_s):
    rows, columns = k_ref.shape[0], k_ref.shape[1]
    tokens = rows * PAD
    fill_rows(k_s, k_ref, rows)
    fill_rows(v_s, v_ref, rows)
    same = same_head()
    for group in range(GROUPS):
        start, wide = span(group)
        lanes = pl.ds(start, LANES)
        k_raw = k_s[:, :, lanes].reshape(tokens, LANES).astype(f32)
        low = jnp.exp(jnp.minimum(k_raw, 0.0))
        feat = jnp.where(k_raw > 0, k_raw + 1.0, low).astype(bf16)
        slope = jnp.where(k_raw > 0, 1.0, low)
        value = v_s[:, :, lanes].reshape(tokens, LANES)
        high, rest = split(expand(received[state_rows(group), :], same))
        ahead = received[head_rows(group), :]
        back = dot(value, high) + dot(value, rest) + ahead[0:1]
        back = (back * slope).reshape(rows, PAD, LANES)
        k_grad[:, :, pl.ds(start, wide)] = back[:, :columns, :wide].astype(bf16)
        here = (dot_nt(feat, high) + dot_nt(feat, rest)).reshape(rows, PAD, LANES)
        here = here + v_local[:, :, lanes]
        v_grad[:, :, pl.ds(start, wide)] = here[:, :columns, :wide].astype(bf16)
        tail = received[tail_rows(group), :]
        for n in range(9):
            term = ahead[n + 1 : n + 2] if n < 7 else tail[n - 7 : n - 6]
            kernel_grad[n // 3, pl.ds(n % 3, 1), pl.ds(start, wide)] = (term * scale)[:, :wide]


def call(body, out_shape, name, scratch=(), plain=(), keep=()):
    def run(*args):
        args = [
            a if n in plain else pltpu.with_memory_space_constraint(a, pltpu.VMEM)
            for n, a in enumerate(args)
        ]
        return pl.pallas_call(
            body,
            out_shape=[
                a if n in keep else pltpu.VMEM(a.shape, a.dtype) for n, a in enumerate(out_shape)
            ],
            in_specs=[pl.BlockSpec(memory_space=pltpu.VMEM)] * len(args),
            out_specs=[pl.BlockSpec(memory_space=pltpu.VMEM)] * len(out_shape),
            scratch_shapes=scratch,
            name=name,
        )(*args)

    return run


def shards(query_input, key_input, value_input, cotangent, local_kernel_weight):
    q, k, v, g = (x[0] for x in (query_input, key_input, value_input, cotangent))
    rows, columns, width = q.shape
    shape = jax.ShapeDtypeStruct
    lanes = GROUPS * LANES
    planes = lax.axis_size("z")
    frames = lax.axis_size("x") * lax.axis_size("c")
    peers = frames * lax.axis_size("y")
    token_scratch = pltpu.VMEM((rows, PAD, lanes), bf16)
    row_scratch = pltpu.VMEM((rows + 1, PAD, lanes), bf16)
    rim_scratch = pltpu.VMEM((rows + 2, PAD, lanes), bf16)
    tokens = shape(q.shape, bf16)
    padded = shape((rows, PAD, lanes), f32)
    edge_shape = shape((2, columns, width), bf16)

    def flat(rows_used):
        return shape((-(-rows_used // peers) * peers, LANES), f32)

    def exchange(x):
        return lax.all_to_all(x, ("x", "c", "y"), 0, 0, tiled=True)

    def scatter(send):
        return exchange(send.reshape(peers, 1, -1))

    def gather(received, body, name, beside, then):
        received, v_now, g_now = lax.optimization_barrier((received, v, g))
        piece = received.shape[1:]
        sums, whole = call(
            totals_kernel, (shape((frames, *piece), f32), shape((planes, *piece), f32)), "totals"
        )(received)
        gathered = lax.all_to_all(whole, "z", 0, 0, tiled=True)
        done = beside(v_now, g_now)
        gathered, done, then = lax.optimization_barrier((gathered, done, then))
        (back,) = call(body, (shape(received.shape, f32),), name)(gathered, sums)
        return exchange(back).reshape(-1, LANES), done, then

    def edge_rows(v, g, row):
        def body(*refs):
            edge_kernel(row, *refs)

        return call(body, (edge_shape,), "edge")(v, g)[0]

    ends = lax.axis_size("y") - 1
    upward = [(i, i + 1) for i in range(ends)]
    downward = [(i + 1, i) for i in range(ends)]
    (send,) = call(
        state_kernel, (flat(STATE_ROWS + GROUPS),), "state", [token_scratch] * 2, plain=(0, 1)
    )(k, v)
    def above_and_terms(v, g):
        above = lax.ppermute(edge_rows(v, g, rows - 1), "y", upward)
        return above, *call(terms_kernel, (shape((16, lanes), f32),), "terms", [row_scratch] * 2)(
            v, g, above
        )

    state, (above, terms), _ = gather(
        scatter(send), prefix_kernel, "prefix", above_and_terms, ()
    )
    (send,) = call(
        query_kernel, (flat(STATE_ROWS + 10 * GROUPS),), "query", [token_scratch] * 2
    )(q, g, state, terms)
    later, _, (q_late, v_late, g_late, state) = gather(
        scatter(send), suffix_kernel, "suffix", lambda v, g: (), (q, v, g, state)
    )
    below = lax.ppermute(edge_rows(v_late, g_late, 0), "y", downward)
    weight = jnp.pad(local_kernel_weight, ((0, 0), (0, 0), (0, lanes - width)))
    q_grad, attn = call(grad_kernel, (tokens, padded), "grad", [token_scratch] * 2, keep=(0,))(
        q_late, g_late, state
    )
    mixed, v_local = call(
        mixed_kernel, (tokens, padded), "mixed", [rim_scratch] * 2, keep=(0,)
    )(v_late, g_late, above, below, weight, attn)
    count = rows * columns
    for axis in ("z", "x", "c", "y"):
        count = count * lax.axis_size(axis)
    scale = 1.0 / math.sqrt(count)

    def key_body(*refs):
        key_kernel(scale, *refs)

    k_grad, v_grad, kernel_grad = call(
        key_body,
        (tokens, tokens, shape(local_kernel_weight.shape, f32)),
        "key",
        [token_scratch] * 2,
        keep=(0, 1, 2),
    )(k, v, later, v_local)
    return (mixed[None], q_grad[None], k_grad[None], v_grad[None], kernel_grad)


def solution(mesh):
    torus = Mesh(mesh.devices.reshape(8, 4, 2, 8), ("z", "x", "c", "y"))
    tokens = P(("z", "x", "c"), "y", None, None)
    return jax.shard_map(
        shards,
        mesh=torus,
        in_specs=(tokens, tokens, tokens, tokens, P()),
        out_specs=(tokens, tokens, tokens, tokens, P()),
        check_vma=False,
    )
```

```python
import math

import jax
import jax.numpy as jnp
from jax import lax
from jax.experimental import pallas as pl
from jax.experimental.pallas import tpu as pltpu
from jax.sharding import Mesh
from jax.sharding import PartitionSpec as P

HEADS = 35
HEAD_DIM = 32
LANES = 128
WIDTH = HEADS * HEAD_DIM
GROUPS = -(-WIDTH // LANES)
PAD = 32
BATCH = 3
STATE_ROWS = GROUPS * HEAD_DIM
TAIL_ROW = STATE_ROWS + 8 * GROUPS

f32 = jnp.float32
bf16 = jnp.bfloat16


def span(group):
    start = group * LANES
    return start, min(LANES, WIDTH - start)


def dot(a, b):
    return lax.dot_general(a, b, (((1,), (0,)), ((), ())), preferred_element_type=f32)


def dot_nt(a, b):
    return lax.dot_general(a, b, (((1,), (1,)), ((), ())), preferred_element_type=f32)


def dot_tn(a, b):
    return lax.dot_general(a, b, (((0,), (0,)), ((), ())), preferred_element_type=f32)


def split(x, axis):
    high = x.astype(bf16)
    return jnp.concatenate([high, (x - high.astype(f32)).astype(bf16)], axis=axis)


def twice(x):
    return jnp.concatenate([x, x], axis=1)


def same_head():
    rows = lax.broadcasted_iota(jnp.int32, (LANES, LANES), 0) // HEAD_DIM
    columns = lax.broadcasted_iota(jnp.int32, (LANES, LANES), 1) // HEAD_DIM
    return rows == columns


def lane_head():
    return lax.broadcasted_iota(jnp.int32, (HEAD_DIM, LANES), 1) // HEAD_DIM


def compact(full, heads):
    out = jnp.zeros((HEAD_DIM, LANES), f32)
    for k in range(LANES // HEAD_DIM):
        out = jnp.where(heads == k, full[k * HEAD_DIM : (k + 1) * HEAD_DIM], out)
    return out


def expand(blocks, same):
    return jnp.where(same, jnp.concatenate([blocks] * (LANES // HEAD_DIM), axis=0), 0.0)


def state_rows(group):
    return pl.ds(group * HEAD_DIM, HEAD_DIM)


def norm_row(group):
    return pl.ds(STATE_ROWS + group, 1)


def head_rows(group, count=8):
    return pl.ds(STATE_ROWS + 8 * group, count)


def tail_rows(group):
    return pl.ds(TAIL_ROW + 2 * group, 2)


def clear_extra(send):
    send[pl.ds(STATE_ROWS, send.shape[0] - STATE_ROWS), :] = jnp.zeros(
        (send.shape[0] - STATE_ROWS, LANES), f32
    )


def batches():
    return [range(n, min(n + BATCH, GROUPS)) for n in range(0, GROUPS, BATCH)]


def fill_rows(scratch, ref, rows):
    scratch[...] = jnp.zeros_like(scratch)
    for r in range(rows):
        scratch[r, pl.ds(0, ref.shape[1]), pl.ds(0, WIDTH)] = ref[r]


def edge_kernel(v_ref, g_ref, first, last):
    rows = v_ref.shape[0]
    for n, ref in enumerate((v_ref, g_ref)):
        first[n] = ref[0]
        last[n] = ref[rows - 1]


def state_kernel(k_ref, v_ref, send, k_s, v_s):
    rows, columns = k_ref.shape[0], k_ref.shape[1]
    fill_rows(k_s, k_ref, rows)
    fill_rows(v_s, v_ref, rows)
    clear_extra(send)
    heads = lane_head()
    token = lax.broadcasted_iota(jnp.int32, (rows, PAD, LANES), 1) < columns
    for groups in batches():
        at = [pl.ds(group * LANES, LANES) for group in groups]
        raw = [k_s[:, :, lanes].astype(f32) for lanes in at]
        feat = [jnp.where(x > 0, x + 1.0, jnp.exp(jnp.minimum(x, 0.0))) for x in raw]
        feat = [jnp.where(token, x, 0.0).astype(bf16).reshape(rows * PAD, LANES) for x in feat]
        value = [v_s[:, :, lanes].reshape(rows * PAD, LANES) for lanes in at]
        whole = [dot_tn(x, y) for x, y in zip(feat, value)]
        for group, x, product in zip(groups, feat, whole):
            send[norm_row(group), :] = jnp.sum(x.astype(f32), axis=0, keepdims=True)
            send[state_rows(group), :] = compact(product, heads)


def totals_kernel(received, frames, send):
    count = frames.shape[0]
    bands = received.shape[0] // count
    whole = jnp.zeros(received.shape[1:], f32)
    for frame in range(count):
        total = received[frame * bands]
        for band in range(1, bands):
            total = total + received[frame * bands + band]
        frames[frame] = total
        whole = whole + total
    for n in range(send.shape[0]):
        send[n] = whole


def prefix_kernel(received, frames, send):
    plane = lax.axis_index("z")
    total = jnp.zeros(received.shape[1:], f32)
    for n in range(received.shape[0]):
        total = total + jnp.where(n < plane, received[n], 0.0)
    count = frames.shape[0]
    bands = send.shape[0] // count
    for frame in range(count):
        total = total + frames[frame]
        for band in range(bands):
            send[frame * bands + band] = total


def suffix_kernel(received, frames, send):
    plane = lax.axis_index("z")
    later = jnp.zeros(received.shape[1:], f32)
    whole = jnp.zeros(received.shape[1:], f32)
    for n in range(received.shape[0]):
        later = later + jnp.where(n > plane, received[n], 0.0)
        whole = whole + received[n]
    lane = lax.broadcasted_iota(jnp.int32, received.shape[1:], 1)
    first = lax.axis_index(("x", "c", "y")) * (received.shape[2] // LANES)
    row = first + lane // LANES
    norm = jnp.logical_and(row < TAIL_ROW, (row - STATE_ROWS) % 8 == 0)
    summed = jnp.logical_and(row >= STATE_ROWS, jnp.logical_not(norm))
    count = frames.shape[0]
    bands = send.shape[0] // count
    for frame in reversed(range(count)):
        later = later + frames[frame]
        out = jnp.where(summed, whole, later)
        for band in range(bands):
            send[frame * bands + band] = out


def fill_rim(scratch, ref, above, below=None):
    rows, columns = ref.shape[0], ref.shape[1]
    scratch[...] = jnp.zeros_like(scratch)
    scratch[0, pl.ds(0, columns), pl.ds(0, WIDTH)] = above
    for r in range(rows):
        scratch[r + 1, pl.ds(0, columns), pl.ds(0, WIDTH)] = ref[r]
    if below is not None:
        scratch[rows + 1, pl.ds(0, columns), pl.ds(0, WIDTH)] = below


def shifted(scratch, lanes):
    out = []
    for r in range(scratch.shape[0]):
        here = scratch[r, :, lanes].astype(f32)
        out.append((pltpu.roll(here, 1, 0), here, pltpu.roll(here, PAD - 1, 0)))
    return out


def terms_kernel(v_ref, g_ref, above, terms, v_s, g_s):
    rows = v_ref.shape[0]
    fill_rim(v_s, v_ref, above[0])
    fill_rim(g_s, g_ref, above[1])
    terms[...] = jnp.zeros_like(terms)
    for group in range(GROUPS):
        lanes = pl.ds(group * LANES, LANES)
        value = shifted(v_s, lanes)
        grad = [g_s[r, :, lanes].astype(f32) for r in range(rows + 1)]
        for n in range(9):
            step = n // 3 - 1
            term = jnp.zeros((PAD, LANES), f32)
            for r in range(1 - max(step, 0), rows + 1 - max(step, 0)):
                term = term + grad[r] * value[r + step][n % 3]
            terms[pl.ds(1 + n, 1), lanes] = jnp.sum(term, axis=0, keepdims=True)


def attend(q_s, g_s, received, groups, same, ones):
    tokens = q_s.shape[0] * PAD
    lane = lax.broadcasted_iota(jnp.int32, (1, LANES), 1)
    at = [pl.ds(group * LANES, LANES) for group in groups]
    raw = [q_s[:, :, lanes].reshape(tokens, LANES).astype(f32) for lanes in at]
    low = [jnp.exp(jnp.minimum(x, 0.0)) for x in raw]
    feat = [jnp.where(x > 0, x + 1.0, y).astype(bf16) for x, y in zip(raw, low)]
    slope = [jnp.where(x > 0, 1.0, y) for x, y in zip(raw, low)]
    grad = [g_s[:, :, lanes].reshape(tokens, LANES) for lanes in at]
    state = [expand(received[state_rows(group), :], same) for group in groups]
    norm = [jnp.where(lane < span(n)[1], received[norm_row(n), :], 1.0) for n in groups]
    den = [dot(split(x.astype(f32) * y, 1), ones) for x, y in zip(feat, norm)]
    num = [dot(twice(x), split(y, 0)) for x, y in zip(feat, state)]
    inverse = [1.0 / x for x in den]
    along = [dot(split(x.astype(f32) * y, 1), ones) for x, y in zip(grad, num)]
    along = [x * y for x, y in zip(along, inverse)]
    return list(zip(groups, feat, slope, grad, state, norm, num, inverse, along))


def query_kernel(q_ref, g_ref, received, terms, send, q_s, g_s):
    rows = q_ref.shape[0]
    fill_rows(q_s, q_ref, rows)
    fill_rows(g_s, g_ref, rows)
    clear_extra(send)
    heads, same = lane_head(), same_head()
    ones = same.astype(f32).astype(bf16)
    ones = jnp.concatenate([ones, ones], axis=0)
    for groups in batches():
        parts = attend(q_s, g_s, received, groups, same, ones)
        scaled = [part[1].astype(f32) * part[7] for part in parts]
        pairs = [dot_tn(part[3], split(x, 1)) for part, x in zip(parts, scaled)]
        for part, x, pair in zip(parts, scaled, pairs):
            group, along = part[0], part[8]
            send[state_rows(group), :] = compact(pair[:, :LANES] + pair[:, LANES:], heads)
            lanes = pl.ds(group * LANES, LANES)
            send[head_rows(group, 8), :] = terms[pl.ds(0, 8), lanes]
            send[head_rows(group, 1), :] = -jnp.sum(x * along, axis=0, keepdims=True)
            send[tail_rows(group), :] = terms[pl.ds(8, 2), lanes]


def grad_kernel(q_ref, g_ref, received, q_grad, attn, q_s, g_s):
    rows, columns = q_ref.shape[0], q_ref.shape[1]
    fill_rows(q_s, q_ref, rows)
    fill_rows(g_s, g_ref, rows)
    same = same_head()
    ones = same.astype(f32).astype(bf16)
    ones = jnp.concatenate([ones, ones], axis=0)
    for groups in batches():
        for group, _, slope, grad, state, norm, num, inverse, along in attend(
            q_s, g_s, received, groups, same, ones
        ):
            start, wide = span(group)
            back = dot_nt(twice(grad), split(state, 1))
            back = ((back - along * norm) * inverse * slope).reshape(rows, PAD, LANES)
            q_grad[:, :, pl.ds(start, wide)] = back[:, :columns, :wide].astype(bf16)
            attn[:, :, pl.ds(start, LANES)] = (num * inverse).reshape(rows, PAD, LANES)


def mixed_kernel(v_ref, g_ref, above, below, w_ref, attn, mixed, v_local, v_s, g_s):
    rows, columns = v_ref.shape[0], v_ref.shape[1]
    fill_rim(v_s, v_ref, above[0], below[0])
    fill_rim(g_s, g_ref, above[1], below[1])
    for group in range(GROUPS):
        start, wide = span(group)
        lanes = pl.ds(start, LANES)
        taps = [
            jnp.broadcast_to(w_ref[n // 3, pl.ds(n % 3, 1), lanes], (PAD, LANES)) for n in range(9)
        ]
        value, grads = shifted(v_s, lanes), shifted(g_s, lanes)
        for r in range(rows):
            here = jnp.zeros((PAD, LANES), f32)
            there = jnp.zeros((PAD, LANES), f32)
            for n, tap in enumerate(taps):
                here = here + tap * value[r + n // 3][n % 3]
                there = there + tap * grads[r + 2 - n // 3][2 - n % 3]
            v_local[r, :, lanes] = there
            here = attn[r, :, lanes] + here
            mixed[r, :, pl.ds(start, wide)] = here[:columns, :wide].astype(bf16)


def key_kernel(scale, k_ref, v_ref, received, v_local, k_grad, v_grad, kernel_grad, k_s, v_s):
    rows, columns = k_ref.shape[0], k_ref.shape[1]
    tokens = rows * PAD
    fill_rows(k_s, k_ref, rows)
    fill_rows(v_s, v_ref, rows)
    same = same_head()
    for groups in batches():
        at = [pl.ds(group * LANES, LANES) for group in groups]
        state = [expand(received[state_rows(group), :], same) for group in groups]
        value = [v_s[:, :, lanes].reshape(tokens, LANES) for lanes in at]
        back = [dot(twice(x), split(y, 0)) for x, y in zip(value, state)]
        raw = [k_s[:, :, lanes].reshape(tokens, LANES).astype(f32) for lanes in at]
        low = [jnp.exp(jnp.minimum(x, 0.0)) for x in raw]
        feat = [jnp.where(x > 0, x + 1.0, y).astype(bf16) for x, y in zip(raw, low)]
        slope = [jnp.where(x > 0, 1.0, y) for x, y in zip(raw, low)]
        forth = [dot_nt(twice(x), split(y, 1)) for x, y in zip(feat, state)]
        for n, group in enumerate(groups):
            start, wide = span(group)
            ahead, tail = received[head_rows(group), :], received[tail_rows(group), :]
            grad = ((back[n] + ahead[0:1]) * slope[n]).reshape(rows, PAD, LANES)
            k_grad[:, :, pl.ds(start, wide)] = grad[:, :columns, :wide].astype(bf16)
            grad = forth[n].reshape(rows, PAD, LANES) + v_local[:, :, at[n]]
            v_grad[:, :, pl.ds(start, wide)] = grad[:, :columns, :wide].astype(bf16)
            for m in range(9):
                term = ahead[m + 1 : m + 2] if m < 7 else tail[m - 7 : m - 6]
                kernel_grad[m // 3, pl.ds(m % 3, 1), pl.ds(start, wide)] = (term * scale)[:, :wide]


def call(body, out_shape, name, scratch=(), plain=(), keep=()):
    def run(*args):
        args = [
            a if n in plain else pltpu.with_memory_space_constraint(a, pltpu.VMEM)
            for n, a in enumerate(args)
        ]
        return pl.pallas_call(
            body,
            out_shape=[
                a if n in keep else pltpu.VMEM(a.shape, a.dtype) for n, a in enumerate(out_shape)
            ],
            in_specs=[pl.BlockSpec(memory_space=pltpu.VMEM)] * len(args),
            out_specs=[pl.BlockSpec(memory_space=pltpu.VMEM)] * len(out_shape),
            scratch_shapes=scratch,
            name=name,
        )(*args)

    return run


def shards(query_input, key_input, value_input, cotangent, local_kernel_weight):
    q, k, v, g = (x[0] for x in (query_input, key_input, value_input, cotangent))
    rows, columns, width = q.shape
    shape = jax.ShapeDtypeStruct
    lanes = GROUPS * LANES
    planes = lax.axis_size("z")
    frames = lax.axis_size("x") * lax.axis_size("c")
    peers = frames * lax.axis_size("y")
    token_scratch = pltpu.VMEM((rows, PAD, lanes), bf16)
    row_scratch = pltpu.VMEM((rows + 1, PAD, lanes), bf16)
    rim_scratch = pltpu.VMEM((rows + 2, PAD, lanes), bf16)
    tokens = shape(q.shape, bf16)
    padded = shape((rows, PAD, lanes), f32)
    edge_shape = shape((2, columns, width), bf16)

    def flat(rows_used):
        return shape((-(-rows_used // peers) * peers, LANES), f32)

    def exchange(x):
        return lax.all_to_all(x, ("x", "c", "y"), 0, 0, tiled=True)

    def scatter(send):
        return exchange(send.reshape(peers, 1, -1))

    def gather(received, body, name, then):
        piece = received.shape[1:]
        sums, whole = call(
            totals_kernel, (shape((frames, *piece), f32), shape((planes, *piece), f32)), "totals"
        )(received)
        gathered = lax.all_to_all(whole, "z", 0, 0, tiled=True)
        gathered, then = lax.optimization_barrier((gathered, then))
        (back,) = call(body, (shape(received.shape, f32),), name)(gathered, sums)
        return exchange(back).reshape(-1, LANES), then

    ends = lax.axis_size("y") - 1
    upward = [(i, i + 1) for i in range(ends)]
    downward = [(i + 1, i) for i in range(ends)]
    first, last = call(edge_kernel, (edge_shape,) * 2, "edges")(v, g)
    above = lax.ppermute(last, "y", upward)
    below = lax.ppermute(first, "y", downward)
    (send,) = call(
        state_kernel, (flat(STATE_ROWS + GROUPS),), "state", [token_scratch] * 2, plain=(0, 1)
    )(k, v)
    received = scatter(send)
    (terms,) = call(terms_kernel, (shape((16, lanes), f32),), "terms", [row_scratch] * 2)(
        v, g, above
    )
    state, (terms, below) = gather(received, prefix_kernel, "prefix", (terms, below))
    (send,) = call(
        query_kernel, (flat(STATE_ROWS + 10 * GROUPS),), "query", [token_scratch] * 2
    )(q, g, state, terms)
    later, (q_late, v_late, g_late, state) = gather(
        scatter(send), suffix_kernel, "suffix", (q, v, g, state)
    )
    weight = jnp.pad(local_kernel_weight, ((0, 0), (0, 0), (0, lanes - width)))
    q_grad, attn = call(grad_kernel, (tokens, padded), "grad", [token_scratch] * 2, keep=(0,))(
        q_late, g_late, state
    )
    mixed, v_local = call(
        mixed_kernel, (tokens, padded), "mixed", [rim_scratch] * 2, keep=(0,)
    )(v_late, g_late, above, below, weight, attn)
    count = rows * columns
    for axis in ("z", "x", "c", "y"):
        count = count * lax.axis_size(axis)
    scale = 1.0 / math.sqrt(count)

    def key_body(*refs):
        key_kernel(scale, *refs)

    k_grad, v_grad, kernel_grad = call(
        key_body,
        (tokens, tokens, shape(local_kernel_weight.shape, f32)),
        "key",
        [token_scratch] * 2,
        keep=(0, 1, 2),
    )(k, v, later, v_local)
    return (mixed[None], q_grad[None], k_grad[None], v_grad[None], kernel_grad)


def solution(mesh):
    torus = Mesh(mesh.devices.reshape(8, 4, 2, 8), ("z", "x", "c", "y"))
    tokens = P(("z", "x", "c"), "y", None, None)
    return jax.shard_map(
        shards,
        mesh=torus,
        in_specs=(tokens, tokens, tokens, tokens, P()),
        out_specs=(tokens, tokens, tokens, tokens, P()),
        check_vma=False,
    )
```

```python
import math

import jax
import jax.numpy as jnp
from jax import lax
from jax.experimental import pallas as pl
from jax.experimental.pallas import tpu as pltpu
from jax.sharding import Mesh
from jax.sharding import PartitionSpec as P

HEADS = 35
HEAD_DIM = 32
LANES = 128
WIDTH = HEADS * HEAD_DIM
GROUPS = -(-WIDTH // LANES)
PAD = 32
BATCH = 5
STATE_ROWS = GROUPS * HEAD_DIM
TAIL_ROW = STATE_ROWS + 8 * GROUPS

f32 = jnp.float32
bf16 = jnp.bfloat16


def span(group):
    start = group * LANES
    return start, min(LANES, WIDTH - start)


def dot(a, b):
    return lax.dot_general(a, b, (((1,), (0,)), ((), ())), preferred_element_type=f32)


def dot_nt(a, b):
    return lax.dot_general(a, b, (((1,), (1,)), ((), ())), preferred_element_type=f32)


def dot_tn(a, b):
    return lax.dot_general(a, b, (((0,), (0,)), ((), ())), preferred_element_type=f32)


def split(x, axis):
    high = x.astype(bf16)
    return jnp.concatenate([high, (x - high.astype(f32)).astype(bf16)], axis=axis)


def twice(x):
    return jnp.concatenate([x, x], axis=1)


def same_head():
    rows = lax.broadcasted_iota(jnp.int32, (LANES, LANES), 0) // HEAD_DIM
    columns = lax.broadcasted_iota(jnp.int32, (LANES, LANES), 1) // HEAD_DIM
    return rows == columns


def lane_head():
    return lax.broadcasted_iota(jnp.int32, (HEAD_DIM, LANES), 1) // HEAD_DIM


def compact(full, heads):
    out = jnp.zeros((HEAD_DIM, LANES), f32)
    for k in range(LANES // HEAD_DIM):
        out = jnp.where(heads == k, full[k * HEAD_DIM : (k + 1) * HEAD_DIM], out)
    return out


def expand(blocks, same):
    return jnp.where(same, jnp.concatenate([blocks] * (LANES // HEAD_DIM), axis=0), 0.0)


def state_rows(group):
    return pl.ds(group * HEAD_DIM, HEAD_DIM)


def norm_row(group):
    return pl.ds(STATE_ROWS + group, 1)


def head_rows(group, count=8):
    return pl.ds(STATE_ROWS + 8 * group, count)


def tail_rows(group):
    return pl.ds(TAIL_ROW + 2 * group, 2)


def clear_extra(send):
    send[pl.ds(STATE_ROWS, send.shape[0] - STATE_ROWS), :] = jnp.zeros(
        (send.shape[0] - STATE_ROWS, LANES), f32
    )


def batches():
    return [range(n, min(n + BATCH, GROUPS)) for n in range(0, GROUPS, BATCH)]


def fill_rows(scratch, ref, rows):
    scratch[...] = jnp.zeros_like(scratch)
    for r in range(rows):
        scratch[r, pl.ds(0, ref.shape[1]), pl.ds(0, WIDTH)] = ref[r]


def edge_kernel(v_ref, g_ref, first, last):
    rows = v_ref.shape[0]
    for n, ref in enumerate((v_ref, g_ref)):
        first[n] = ref[0]
        last[n] = ref[rows - 1]


def state_kernel(k_ref, v_ref, send, k_s, v_s):
    rows, columns = k_ref.shape[0], k_ref.shape[1]
    fill_rows(k_s, k_ref, rows)
    fill_rows(v_s, v_ref, rows)
    clear_extra(send)
    heads = lane_head()
    token = lax.broadcasted_iota(jnp.int32, (rows, PAD, LANES), 1) < columns
    for groups in batches():
        at = [pl.ds(group * LANES, LANES) for group in groups]
        raw = [k_s[:, :, lanes].astype(f32) for lanes in at]
        feat = [jnp.where(x > 0, x + 1.0, jnp.exp(jnp.minimum(x, 0.0))) for x in raw]
        feat = [jnp.where(token, x, 0.0).astype(bf16).reshape(rows * PAD, LANES) for x in feat]
        value = [v_s[:, :, lanes].reshape(rows * PAD, LANES) for lanes in at]
        whole = [dot_tn(x, y) for x, y in zip(feat, value)]
        for group, x, product in zip(groups, feat, whole):
            send[norm_row(group), :] = jnp.sum(x.astype(f32), axis=0, keepdims=True)
            send[state_rows(group), :] = compact(product, heads)


def totals_kernel(received, frames, send):
    count = frames.shape[0]
    bands = received.shape[0] // count
    whole = jnp.zeros(received.shape[1:], f32)
    for frame in range(count):
        total = received[frame * bands]
        for band in range(1, bands):
            total = total + received[frame * bands + band]
        frames[frame] = total
        whole = whole + total
    for n in range(send.shape[0]):
        send[n] = whole


def prefix_kernel(received, frames, send):
    plane = lax.axis_index("z")
    total = jnp.zeros(received.shape[1:], f32)
    for n in range(received.shape[0]):
        total = total + jnp.where(n < plane, received[n], 0.0)
    count = frames.shape[0]
    bands = send.shape[0] // count
    for frame in range(count):
        total = total + frames[frame]
        for band in range(bands):
            send[frame * bands + band] = total


def suffix_kernel(received, frames, send):
    plane = lax.axis_index("z")
    later = jnp.zeros(received.shape[1:], f32)
    whole = jnp.zeros(received.shape[1:], f32)
    for n in range(received.shape[0]):
        later = later + jnp.where(n > plane, received[n], 0.0)
        whole = whole + received[n]
    lane = lax.broadcasted_iota(jnp.int32, received.shape[1:], 1)
    first = lax.axis_index(("x", "c", "y")) * (received.shape[2] // LANES)
    row = first + lane // LANES
    norm = jnp.logical_and(row < TAIL_ROW, (row - STATE_ROWS) % 8 == 0)
    summed = jnp.logical_and(row >= STATE_ROWS, jnp.logical_not(norm))
    count = frames.shape[0]
    bands = send.shape[0] // count
    for frame in reversed(range(count)):
        later = later + frames[frame]
        out = jnp.where(summed, whole, later)
        for band in range(bands):
            send[frame * bands + band] = out


def fill_rim(scratch, ref, above, below=None):
    rows, columns = ref.shape[0], ref.shape[1]
    scratch[...] = jnp.zeros_like(scratch)
    scratch[0, pl.ds(0, columns), pl.ds(0, WIDTH)] = above
    for r in range(rows):
        scratch[r + 1, pl.ds(0, columns), pl.ds(0, WIDTH)] = ref[r]
    if below is not None:
        scratch[rows + 1, pl.ds(0, columns), pl.ds(0, WIDTH)] = below


def shifted(scratch, lanes):
    out = []
    for r in range(scratch.shape[0]):
        here = scratch[r, :, lanes].astype(f32)
        out.append((pltpu.roll(here, 1, 0), here, pltpu.roll(here, PAD - 1, 0)))
    return out


def terms_kernel(v_ref, g_ref, above, terms, v_s, g_s):
    rows = v_ref.shape[0]
    fill_rim(v_s, v_ref, above[0])
    fill_rim(g_s, g_ref, above[1])
    terms[...] = jnp.zeros_like(terms)
    for group in range(GROUPS):
        lanes = pl.ds(group * LANES, LANES)
        value = shifted(v_s, lanes)
        grad = [g_s[r, :, lanes].astype(f32) for r in range(rows + 1)]
        for n in range(9):
            step = n // 3 - 1
            term = jnp.zeros((PAD, LANES), f32)
            for r in range(1 - max(step, 0), rows + 1 - max(step, 0)):
                term = term + grad[r] * value[r + step][n % 3]
            terms[pl.ds(1 + n, 1), lanes] = jnp.sum(term, axis=0, keepdims=True)


def attend(q_s, g_s, received, groups, same, ones):
    tokens = q_s.shape[0] * PAD
    lane = lax.broadcasted_iota(jnp.int32, (1, LANES), 1)
    at = [pl.ds(group * LANES, LANES) for group in groups]
    raw = [q_s[:, :, lanes].reshape(tokens, LANES).astype(f32) for lanes in at]
    low = [jnp.exp(jnp.minimum(x, 0.0)) for x in raw]
    feat = [jnp.where(x > 0, x + 1.0, y).astype(bf16) for x, y in zip(raw, low)]
    slope = [jnp.where(x > 0, 1.0, y) for x, y in zip(raw, low)]
    grad = [g_s[:, :, lanes].reshape(tokens, LANES) for lanes in at]
    state = [expand(received[state_rows(group), :], same) for group in groups]
    norm = [jnp.where(lane < span(n)[1], received[norm_row(n), :], 1.0) for n in groups]
    den = [dot(split(x.astype(f32) * y, 1), ones) for x, y in zip(feat, norm)]
    num = [dot(twice(x), split(y, 0)) for x, y in zip(feat, state)]
    inverse = [1.0 / x for x in den]
    along = [dot(split(x.astype(f32) * y, 1), ones) for x, y in zip(grad, num)]
    along = [x * y for x, y in zip(along, inverse)]
    return list(zip(groups, feat, slope, grad, state, norm, num, inverse, along))


def query_kernel(q_ref, g_ref, received, terms, send, q_s, g_s):
    rows = q_ref.shape[0]
    fill_rows(q_s, q_ref, rows)
    fill_rows(g_s, g_ref, rows)
    clear_extra(send)
    heads, same = lane_head(), same_head()
    ones = same.astype(f32).astype(bf16)
    ones = jnp.concatenate([ones, ones], axis=0)
    for groups in batches():
        parts = attend(q_s, g_s, received, groups, same, ones)
        scaled = [part[1].astype(f32) * part[7] for part in parts]
        pairs = [dot_tn(part[3], split(x, 1)) for part, x in zip(parts, scaled)]
        for part, x, pair in zip(parts, scaled, pairs):
            group, along = part[0], part[8]
            send[state_rows(group), :] = compact(pair[:, :LANES] + pair[:, LANES:], heads)
            lanes = pl.ds(group * LANES, LANES)
            send[head_rows(group, 8), :] = terms[pl.ds(0, 8), lanes]
            send[head_rows(group, 1), :] = -jnp.sum(x * along, axis=0, keepdims=True)
            send[tail_rows(group), :] = terms[pl.ds(8, 2), lanes]


def grad_kernel(q_ref, g_ref, received, q_grad, attn, q_s, g_s):
    rows, columns = q_ref.shape[0], q_ref.shape[1]
    fill_rows(q_s, q_ref, rows)
    fill_rows(g_s, g_ref, rows)
    same = same_head()
    ones = same.astype(f32).astype(bf16)
    ones = jnp.concatenate([ones, ones], axis=0)
    for groups in batches():
        for group, _, slope, grad, state, norm, num, inverse, along in attend(
            q_s, g_s, received, groups, same, ones
        ):
            start, wide = span(group)
            back = dot_nt(twice(grad), split(state, 1))
            back = ((back - along * norm) * inverse * slope).reshape(rows, PAD, LANES)
            q_grad[:, :, pl.ds(start, wide)] = back[:, :columns, :wide].astype(bf16)
            attn[:, :, pl.ds(start, LANES)] = (num * inverse).reshape(rows, PAD, LANES)


def mixed_kernel(v_ref, g_ref, above, below, w_ref, attn, mixed, v_local, v_s, g_s):
    rows, columns = v_ref.shape[0], v_ref.shape[1]
    fill_rim(v_s, v_ref, above[0], below[0])
    fill_rim(g_s, g_ref, above[1], below[1])
    for group in range(GROUPS):
        start, wide = span(group)
        lanes = pl.ds(start, LANES)
        taps = [
            jnp.broadcast_to(w_ref[n // 3, pl.ds(n % 3, 1), lanes], (PAD, LANES)) for n in range(9)
        ]
        value, grads = shifted(v_s, lanes), shifted(g_s, lanes)
        for r in range(rows):
            here = jnp.zeros((PAD, LANES), f32)
            there = jnp.zeros((PAD, LANES), f32)
            for n, tap in enumerate(taps):
                here = here + tap * value[r + n // 3][n % 3]
                there = there + tap * grads[r + 2 - n // 3][2 - n % 3]
            v_local[r, :, lanes] = there
            here = attn[r, :, lanes] + here
            mixed[r, :, pl.ds(start, wide)] = here[:columns, :wide].astype(bf16)


def key_kernel(scale, k_ref, v_ref, received, v_local, k_grad, v_grad, kernel_grad, k_s, v_s):
    rows, columns = k_ref.shape[0], k_ref.shape[1]
    tokens = rows * PAD
    fill_rows(k_s, k_ref, rows)
    fill_rows(v_s, v_ref, rows)
    same = same_head()
    for groups in batches():
        at = [pl.ds(group * LANES, LANES) for group in groups]
        state = [expand(received[state_rows(group), :], same) for group in groups]
        value = [v_s[:, :, lanes].reshape(tokens, LANES) for lanes in at]
        back = [dot(twice(x), split(y, 0)) for x, y in zip(value, state)]
        raw = [k_s[:, :, lanes].reshape(tokens, LANES).astype(f32) for lanes in at]
        low = [jnp.exp(jnp.minimum(x, 0.0)) for x in raw]
        feat = [jnp.where(x > 0, x + 1.0, y).astype(bf16) for x, y in zip(raw, low)]
        slope = [jnp.where(x > 0, 1.0, y) for x, y in zip(raw, low)]
        forth = [dot_nt(twice(x), split(y, 1)) for x, y in zip(feat, state)]
        for n, group in enumerate(groups):
            start, wide = span(group)
            ahead, tail = received[head_rows(group), :], received[tail_rows(group), :]
            grad = ((back[n] + ahead[0:1]) * slope[n]).reshape(rows, PAD, LANES)
            k_grad[:, :, pl.ds(start, wide)] = grad[:, :columns, :wide].astype(bf16)
            grad = forth[n].reshape(rows, PAD, LANES) + v_local[:, :, at[n]]
            v_grad[:, :, pl.ds(start, wide)] = grad[:, :columns, :wide].astype(bf16)
            for m in range(9):
                term = ahead[m + 1 : m + 2] if m < 7 else tail[m - 7 : m - 6]
                kernel_grad[m // 3, pl.ds(m % 3, 1), pl.ds(start, wide)] = (term * scale)[:, :wide]


def call(body, out_shape, name, scratch=(), plain=(), keep=()):
    def run(*args):
        args = [
            a if n in plain else pltpu.with_memory_space_constraint(a, pltpu.VMEM)
            for n, a in enumerate(args)
        ]
        return pl.pallas_call(
            body,
            out_shape=[
                a if n in keep else pltpu.VMEM(a.shape, a.dtype) for n, a in enumerate(out_shape)
            ],
            in_specs=[pl.BlockSpec(memory_space=pltpu.VMEM)] * len(args),
            out_specs=[pl.BlockSpec(memory_space=pltpu.VMEM)] * len(out_shape),
            scratch_shapes=scratch,
            name=name,
        )(*args)

    return run


def shards(query_input, key_input, value_input, cotangent, local_kernel_weight):
    q, k, v, g = (x[0] for x in (query_input, key_input, value_input, cotangent))
    rows, columns, width = q.shape
    shape = jax.ShapeDtypeStruct
    lanes = GROUPS * LANES
    planes = lax.axis_size("z")
    frames = lax.axis_size("x") * lax.axis_size("c")
    peers = frames * lax.axis_size("y")
    token_scratch = pltpu.VMEM((rows, PAD, lanes), bf16)
    row_scratch = pltpu.VMEM((rows + 1, PAD, lanes), bf16)
    rim_scratch = pltpu.VMEM((rows + 2, PAD, lanes), bf16)
    tokens = shape(q.shape, bf16)
    padded = shape((rows, PAD, lanes), f32)
    edge_shape = shape((2, columns, width), bf16)

    def flat(rows_used):
        return shape((-(-rows_used // peers) * peers, LANES), f32)

    def exchange(x):
        return lax.all_to_all(x, ("x", "c", "y"), 0, 0, tiled=True)

    def scatter(send):
        return exchange(send.reshape(peers, 1, -1))

    def gather(received, body, name, then):
        piece = received.shape[1:]
        sums, whole = call(
            totals_kernel, (shape((frames, *piece), f32), shape((planes, *piece), f32)), "totals"
        )(received)
        gathered = lax.all_to_all(whole, "z", 0, 0, tiled=True)
        gathered, then = lax.optimization_barrier((gathered, then))
        (back,) = call(body, (shape(received.shape, f32),), name)(gathered, sums)
        return exchange(back).reshape(-1, LANES), then

    ends = lax.axis_size("y") - 1
    upward = [(i, i + 1) for i in range(ends)]
    downward = [(i + 1, i) for i in range(ends)]
    first, last = call(edge_kernel, (edge_shape,) * 2, "edges")(v, g)
    above = lax.ppermute(last, "y", upward)
    below = lax.ppermute(first, "y", downward)
    (send,) = call(
        state_kernel, (flat(STATE_ROWS + GROUPS),), "state", [token_scratch] * 2, plain=(0, 1)
    )(k, v)
    received = scatter(send)
    (terms,) = call(terms_kernel, (shape((16, lanes), f32),), "terms", [row_scratch] * 2)(
        v, g, above
    )
    state, (terms, below) = gather(received, prefix_kernel, "prefix", (terms, below))
    (send,) = call(
        query_kernel, (flat(STATE_ROWS + 10 * GROUPS),), "query", [token_scratch] * 2
    )(q, g, state, terms)
    later, (q_late, v_late, g_late, state) = gather(
        scatter(send), suffix_kernel, "suffix", (q, v, g, state)
    )
    weight = jnp.pad(local_kernel_weight, ((0, 0), (0, 0), (0, lanes - width)))
    q_grad, attn = call(grad_kernel, (tokens, padded), "grad", [token_scratch] * 2, keep=(0,))(
        q_late, g_late, state
    )
    mixed, v_local = call(
        mixed_kernel, (tokens, padded), "mixed", [rim_scratch] * 2, keep=(0,)
    )(v_late, g_late, above, below, weight, attn)
    count = rows * columns
    for axis in ("z", "x", "c", "y"):
        count = count * lax.axis_size(axis)
    scale = 1.0 / math.sqrt(count)

    def key_body(*refs):
        key_kernel(scale, *refs)

    k_grad, v_grad, kernel_grad = call(
        key_body,
        (tokens, tokens, shape(local_kernel_weight.shape, f32)),
        "key",
        [token_scratch] * 2,
        keep=(0, 1, 2),
    )(k, v, later, v_local)
    return (mixed[None], q_grad[None], k_grad[None], v_grad[None], kernel_grad)


def solution(mesh):
    torus = Mesh(mesh.devices.reshape(8, 4, 2, 8), ("z", "x", "c", "y"))
    tokens = P(("z", "x", "c"), "y", None, None)
    return jax.shard_map(
        shards,
        mesh=torus,
        in_specs=(tokens, tokens, tokens, tokens, P()),
        out_specs=(tokens, tokens, tokens, tokens, P()),
        check_vma=False,
    )
```

```python
import math

import jax
import jax.numpy as jnp
from jax import lax
from jax.experimental import pallas as pl
from jax.experimental.pallas import tpu as pltpu
from jax.sharding import Mesh
from jax.sharding import PartitionSpec as P

HEADS = 35
HEAD_DIM = 32
LANES = 128
WIDTH = HEADS * HEAD_DIM
GROUPS = -(-WIDTH // LANES)
PAD = 32
BATCH = 5
STATE_ROWS = GROUPS * HEAD_DIM
TAIL_ROW = STATE_ROWS + 8 * GROUPS

f32 = jnp.float32
bf16 = jnp.bfloat16


def span(group):
    start = group * LANES
    return start, min(LANES, WIDTH - start)


def dot(a, b):
    return lax.dot_general(a, b, (((1,), (0,)), ((), ())), preferred_element_type=f32)


def dot_nt(a, b):
    return lax.dot_general(a, b, (((1,), (1,)), ((), ())), preferred_element_type=f32)


def dot_tn(a, b):
    return lax.dot_general(a, b, (((0,), (0,)), ((), ())), preferred_element_type=f32)


def split(x, axis):
    high = x.astype(bf16)
    return jnp.concatenate([high, (x - high.astype(f32)).astype(bf16)], axis=axis)


def twice(x):
    return jnp.concatenate([x, x], axis=1)


def same_head():
    rows = lax.broadcasted_iota(jnp.int32, (LANES, LANES), 0) // HEAD_DIM
    columns = lax.broadcasted_iota(jnp.int32, (LANES, LANES), 1) // HEAD_DIM
    return rows == columns


def lane_head():
    return lax.broadcasted_iota(jnp.int32, (HEAD_DIM, LANES), 1) // HEAD_DIM


def compact(full, heads):
    out = jnp.zeros((HEAD_DIM, LANES), f32)
    for k in range(LANES // HEAD_DIM):
        out = jnp.where(heads == k, full[k * HEAD_DIM : (k + 1) * HEAD_DIM], out)
    return out


def expand(blocks, same):
    return jnp.where(same, jnp.concatenate([blocks] * (LANES // HEAD_DIM), axis=0), 0.0)


def state_rows(group):
    return pl.ds(group * HEAD_DIM, HEAD_DIM)


def norm_row(group):
    return pl.ds(STATE_ROWS + group, 1)


def head_rows(group, count=8):
    return pl.ds(STATE_ROWS + 8 * group, count)


def tail_rows(group):
    return pl.ds(TAIL_ROW + 2 * group, 2)


def clear_extra(send):
    send[pl.ds(STATE_ROWS, send.shape[0] - STATE_ROWS), :] = jnp.zeros(
        (send.shape[0] - STATE_ROWS, LANES), f32
    )


def batches():
    return [range(n, min(n + BATCH, GROUPS)) for n in range(0, GROUPS, BATCH)]


def fill_rows(scratch, ref, rows):
    scratch[...] = jnp.zeros_like(scratch)
    for r in range(rows):
        scratch[r, pl.ds(0, ref.shape[1]), pl.ds(0, WIDTH)] = ref[r]


def edge_kernel(v_ref, g_ref, first, last):
    rows = v_ref.shape[0]
    for n, ref in enumerate((v_ref, g_ref)):
        first[n] = ref[0]
        last[n] = ref[rows - 1]


def state_kernel(k_ref, v_ref, send, k_s, v_s):
    rows, columns = k_ref.shape[0], k_ref.shape[1]
    fill_rows(k_s, k_ref, rows)
    fill_rows(v_s, v_ref, rows)
    clear_extra(send)
    heads = lane_head()
    token = lax.broadcasted_iota(jnp.int32, (rows, PAD, LANES), 1) < columns
    for groups in batches():
        at = [pl.ds(group * LANES, LANES) for group in groups]
        raw = [k_s[:, :, lanes].astype(f32) for lanes in at]
        feat = [jnp.where(x > 0, x + 1.0, jnp.exp(jnp.minimum(x, 0.0))) for x in raw]
        feat = [jnp.where(token, x, 0.0).astype(bf16).reshape(rows * PAD, LANES) for x in feat]
        value = [v_s[:, :, lanes].reshape(rows * PAD, LANES) for lanes in at]
        whole = [dot_tn(x, y) for x, y in zip(feat, value)]
        for group, x, product in zip(groups, feat, whole):
            send[norm_row(group), :] = jnp.sum(x.astype(f32), axis=0, keepdims=True)
            send[state_rows(group), :] = compact(product, heads)


def totals_kernel(received, frames, send):
    count = frames.shape[0]
    bands = received.shape[0] // count
    whole = jnp.zeros(received.shape[1:], f32)
    for frame in range(count):
        total = received[frame]
        for band in range(1, bands):
            total = total + received[band * count + frame]
        frames[frame] = total
        whole = whole + total
    for n in range(send.shape[0]):
        send[n] = whole


def prefix_kernel(received, frames, send):
    plane = lax.axis_index("z")
    total = jnp.zeros(received.shape[1:], f32)
    for n in range(received.shape[0]):
        total = total + jnp.where(n < plane, received[n], 0.0)
    count = frames.shape[0]
    bands = send.shape[0] // count
    for frame in range(count):
        total = total + frames[frame]
        for band in range(bands):
            send[band * count + frame] = total


def suffix_kernel(received, frames, send):
    plane = lax.axis_index("z")
    later = jnp.zeros(received.shape[1:], f32)
    whole = jnp.zeros(received.shape[1:], f32)
    for n in range(received.shape[0]):
        later = later + jnp.where(n > plane, received[n], 0.0)
        whole = whole + received[n]
    lane = lax.broadcasted_iota(jnp.int32, received.shape[1:], 1)
    first = lax.axis_index(("y", "x", "c")) * (received.shape[2] // LANES)
    row = first + lane // LANES
    norm = jnp.logical_and(row < TAIL_ROW, (row - STATE_ROWS) % 8 == 0)
    summed = jnp.logical_and(row >= STATE_ROWS, jnp.logical_not(norm))
    count = frames.shape[0]
    bands = send.shape[0] // count
    for frame in reversed(range(count)):
        later = later + frames[frame]
        out = jnp.where(summed, whole, later)
        for band in range(bands):
            send[band * count + frame] = out


def fill_rim(scratch, ref, above, below=None):
    rows, columns = ref.shape[0], ref.shape[1]
    scratch[...] = jnp.zeros_like(scratch)
    scratch[0, pl.ds(0, columns), pl.ds(0, WIDTH)] = above
    for r in range(rows):
        scratch[r + 1, pl.ds(0, columns), pl.ds(0, WIDTH)] = ref[r]
    if below is not None:
        scratch[rows + 1, pl.ds(0, columns), pl.ds(0, WIDTH)] = below


def shifted(scratch, lanes):
    out = []
    for r in range(scratch.shape[0]):
        here = scratch[r, :, lanes].astype(f32)
        out.append((pltpu.roll(here, 1, 0), here, pltpu.roll(here, PAD - 1, 0)))
    return out


def terms_kernel(v_ref, g_ref, above, terms, v_s, g_s):
    rows = v_ref.shape[0]
    fill_rim(v_s, v_ref, above[0])
    fill_rim(g_s, g_ref, above[1])
    terms[...] = jnp.zeros_like(terms)
    for group in range(GROUPS):
        lanes = pl.ds(group * LANES, LANES)
        value = shifted(v_s, lanes)
        grad = [g_s[r, :, lanes].astype(f32) for r in range(rows + 1)]
        for n in range(9):
            step = n // 3 - 1
            term = jnp.zeros((PAD, LANES), f32)
            for r in range(1 - max(step, 0), rows + 1 - max(step, 0)):
                term = term + grad[r] * value[r + step][n % 3]
            terms[pl.ds(1 + n, 1), lanes] = jnp.sum(term, axis=0, keepdims=True)


def attend(q_s, g_s, received, groups, same, ones):
    tokens = q_s.shape[0] * PAD
    lane = lax.broadcasted_iota(jnp.int32, (1, LANES), 1)
    at = [pl.ds(group * LANES, LANES) for group in groups]
    raw = [q_s[:, :, lanes].reshape(tokens, LANES).astype(f32) for lanes in at]
    low = [jnp.exp(jnp.minimum(x, 0.0)) for x in raw]
    feat = [jnp.where(x > 0, x + 1.0, y).astype(bf16) for x, y in zip(raw, low)]
    slope = [jnp.where(x > 0, 1.0, y) for x, y in zip(raw, low)]
    grad = [g_s[:, :, lanes].reshape(tokens, LANES) for lanes in at]
    state = [expand(received[state_rows(group), :], same) for group in groups]
    norm = [jnp.where(lane < span(n)[1], received[norm_row(n), :], 1.0) for n in groups]
    den = [dot(split(x.astype(f32) * y, 1), ones) for x, y in zip(feat, norm)]
    num = [dot(twice(x), split(y, 0)) for x, y in zip(feat, state)]
    inverse = [1.0 / x for x in den]
    along = [dot(split(x.astype(f32) * y, 1), ones) for x, y in zip(grad, num)]
    along = [x * y for x, y in zip(along, inverse)]
    return list(zip(groups, feat, slope, grad, state, norm, num, inverse, along))


def query_kernel(q_ref, g_ref, received, terms, send, q_s, g_s):
    rows = q_ref.shape[0]
    fill_rows(q_s, q_ref, rows)
    fill_rows(g_s, g_ref, rows)
    clear_extra(send)
    heads, same = lane_head(), same_head()
    ones = same.astype(f32).astype(bf16)
    ones = jnp.concatenate([ones, ones], axis=0)
    for groups in batches():
        parts = attend(q_s, g_s, received, groups, same, ones)
        scaled = [part[1].astype(f32) * part[7] for part in parts]
        pairs = [dot_tn(part[3], split(x, 1)) for part, x in zip(parts, scaled)]
        for part, x, pair in zip(parts, scaled, pairs):
            group, along = part[0], part[8]
            send[state_rows(group), :] = compact(pair[:, :LANES] + pair[:, LANES:], heads)
            lanes = pl.ds(group * LANES, LANES)
            send[head_rows(group, 8), :] = terms[pl.ds(0, 8), lanes]
            send[head_rows(group, 1), :] = -jnp.sum(x * along, axis=0, keepdims=True)
            send[tail_rows(group), :] = terms[pl.ds(8, 2), lanes]


def grad_kernel(q_ref, g_ref, received, q_grad, attn, q_s, g_s):
    rows, columns = q_ref.shape[0], q_ref.shape[1]
    fill_rows(q_s, q_ref, rows)
    fill_rows(g_s, g_ref, rows)
    same = same_head()
    ones = same.astype(f32).astype(bf16)
    ones = jnp.concatenate([ones, ones], axis=0)
    for groups in batches():
        for group, _, slope, grad, state, norm, num, inverse, along in attend(
            q_s, g_s, received, groups, same, ones
        ):
            start, wide = span(group)
            back = dot_nt(twice(grad), split(state, 1))
            back = ((back - along * norm) * inverse * slope).reshape(rows, PAD, LANES)
            q_grad[:, :, pl.ds(start, wide)] = back[:, :columns, :wide].astype(bf16)
            attn[:, :, pl.ds(start, LANES)] = (num * inverse).reshape(rows, PAD, LANES)


def mixed_kernel(v_ref, g_ref, above, below, w_ref, attn, mixed, v_local, v_s, g_s):
    rows, columns = v_ref.shape[0], v_ref.shape[1]
    fill_rim(v_s, v_ref, above[0], below[0])
    fill_rim(g_s, g_ref, above[1], below[1])
    for group in range(GROUPS):
        start, wide = span(group)
        lanes = pl.ds(start, LANES)
        taps = [
            jnp.broadcast_to(w_ref[n // 3, pl.ds(n % 3, 1), lanes], (PAD, LANES)) for n in range(9)
        ]
        value, grads = shifted(v_s, lanes), shifted(g_s, lanes)
        for r in range(rows):
            here = jnp.zeros((PAD, LANES), f32)
            there = jnp.zeros((PAD, LANES), f32)
            for n, tap in enumerate(taps):
                here = here + tap * value[r + n // 3][n % 3]
                there = there + tap * grads[r + 2 - n // 3][2 - n % 3]
            v_local[r, :, lanes] = there
            here = attn[r, :, lanes] + here
            mixed[r, :, pl.ds(start, wide)] = here[:columns, :wide].astype(bf16)


def key_kernel(scale, k_ref, v_ref, received, v_local, k_grad, v_grad, kernel_grad, k_s, v_s):
    rows, columns = k_ref.shape[0], k_ref.shape[1]
    tokens = rows * PAD
    fill_rows(k_s, k_ref, rows)
    fill_rows(v_s, v_ref, rows)
    same = same_head()
    for groups in batches():
        at = [pl.ds(group * LANES, LANES) for group in groups]
        state = [expand(received[state_rows(group), :], same) for group in groups]
        value = [v_s[:, :, lanes].reshape(tokens, LANES) for lanes in at]
        back = [dot(twice(x), split(y, 0)) for x, y in zip(value, state)]
        raw = [k_s[:, :, lanes].reshape(tokens, LANES).astype(f32) for lanes in at]
        low = [jnp.exp(jnp.minimum(x, 0.0)) for x in raw]
        feat = [jnp.where(x > 0, x + 1.0, y).astype(bf16) for x, y in zip(raw, low)]
        slope = [jnp.where(x > 0, 1.0, y) for x, y in zip(raw, low)]
        forth = [dot_nt(twice(x), split(y, 1)) for x, y in zip(feat, state)]
        for n, group in enumerate(groups):
            start, wide = span(group)
            ahead, tail = received[head_rows(group), :], received[tail_rows(group), :]
            grad = ((back[n] + ahead[0:1]) * slope[n]).reshape(rows, PAD, LANES)
            k_grad[:, :, pl.ds(start, wide)] = grad[:, :columns, :wide].astype(bf16)
            grad = forth[n].reshape(rows, PAD, LANES) + v_local[:, :, at[n]]
            v_grad[:, :, pl.ds(start, wide)] = grad[:, :columns, :wide].astype(bf16)
            for m in range(9):
                term = ahead[m + 1 : m + 2] if m < 7 else tail[m - 7 : m - 6]
                kernel_grad[m // 3, pl.ds(m % 3, 1), pl.ds(start, wide)] = (term * scale)[:, :wide]


def call(body, out_shape, name, scratch=(), plain=(), keep=()):
    def run(*args):
        args = [
            a if n in plain else pltpu.with_memory_space_constraint(a, pltpu.VMEM)
            for n, a in enumerate(args)
        ]
        return pl.pallas_call(
            body,
            out_shape=[
                a if n in keep else pltpu.VMEM(a.shape, a.dtype) for n, a in enumerate(out_shape)
            ],
            in_specs=[pl.BlockSpec(memory_space=pltpu.VMEM)] * len(args),
            out_specs=[pl.BlockSpec(memory_space=pltpu.VMEM)] * len(out_shape),
            scratch_shapes=scratch,
            name=name,
        )(*args)

    return run


def shards(query_input, key_input, value_input, cotangent, local_kernel_weight):
    q, k, v, g = (x[0] for x in (query_input, key_input, value_input, cotangent))
    rows, columns, width = q.shape
    shape = jax.ShapeDtypeStruct
    lanes = GROUPS * LANES
    planes = lax.axis_size("z")
    frames = lax.axis_size("x") * lax.axis_size("c")
    peers = frames * lax.axis_size("y")
    token_scratch = pltpu.VMEM((rows, PAD, lanes), bf16)
    row_scratch = pltpu.VMEM((rows + 1, PAD, lanes), bf16)
    rim_scratch = pltpu.VMEM((rows + 2, PAD, lanes), bf16)
    tokens = shape(q.shape, bf16)
    padded = shape((rows, PAD, lanes), f32)
    edge_shape = shape((2, columns, width), bf16)

    def flat(rows_used):
        return shape((-(-rows_used // peers) * peers, LANES), f32)

    def exchange(x):
        return lax.all_to_all(x, ("y", "x", "c"), 0, 0, tiled=True)

    def scatter(send):
        return exchange(send.reshape(peers, 1, -1))

    def gather(received, body, name, then):
        piece = received.shape[1:]
        sums, whole = call(
            totals_kernel, (shape((frames, *piece), f32), shape((planes, *piece), f32)), "totals"
        )(received)
        gathered = lax.all_to_all(whole, "z", 0, 0, tiled=True)
        gathered, then = lax.optimization_barrier((gathered, then))
        (back,) = call(body, (shape(received.shape, f32),), name)(gathered, sums)
        return exchange(back).reshape(-1, LANES), then

    ends = lax.axis_size("y") - 1
    upward = [(i, i + 1) for i in range(ends)]
    downward = [(i + 1, i) for i in range(ends)]
    first, last = call(edge_kernel, (edge_shape,) * 2, "edges")(v, g)
    above = lax.ppermute(last, "y", upward)
    below = lax.ppermute(first, "y", downward)
    (send,) = call(
        state_kernel, (flat(STATE_ROWS + GROUPS),), "state", [token_scratch] * 2, plain=(0, 1)
    )(k, v)
    received = scatter(send)
    (terms,) = call(terms_kernel, (shape((16, lanes), f32),), "terms", [row_scratch] * 2)(
        v, g, above
    )
    state, (terms, below) = gather(received, prefix_kernel, "prefix", (terms, below))
    (send,) = call(
        query_kernel, (flat(STATE_ROWS + 10 * GROUPS),), "query", [token_scratch] * 2
    )(q, g, state, terms)
    later, (q_late, v_late, g_late, state) = gather(
        scatter(send), suffix_kernel, "suffix", (q, v, g, state)
    )
    weight = jnp.pad(local_kernel_weight, ((0, 0), (0, 0), (0, lanes - width)))
    q_grad, attn = call(grad_kernel, (tokens, padded), "grad", [token_scratch] * 2, keep=(0,))(
        q_late, g_late, state
    )
    mixed, v_local = call(
        mixed_kernel, (tokens, padded), "mixed", [rim_scratch] * 2, keep=(0,)
    )(v_late, g_late, above, below, weight, attn)
    count = rows * columns
    for axis in ("z", "x", "c", "y"):
        count = count * lax.axis_size(axis)
    scale = 1.0 / math.sqrt(count)

    def key_body(*refs):
        key_kernel(scale, *refs)

    k_grad, v_grad, kernel_grad = call(
        key_body,
        (tokens, tokens, shape(local_kernel_weight.shape, f32)),
        "key",
        [token_scratch] * 2,
        keep=(0, 1, 2),
    )(k, v, later, v_local)
    return (mixed[None], q_grad[None], k_grad[None], v_grad[None], kernel_grad)


def solution(mesh):
    torus = Mesh(mesh.devices.reshape(8, 4, 2, 8), ("z", "x", "c", "y"))
    tokens = P(("z", "x", "c"), "y", None, None)
    return jax.shard_map(
        shards,
        mesh=torus,
        in_specs=(tokens, tokens, tokens, tokens, P()),
        out_specs=(tokens, tokens, tokens, tokens, P()),
        check_vma=False,
    )
```
